768 devices in a mesh: dp: 64 (over z_hi, y, core), neg: 12 (over z_lo, x).
Axes of the slice: x: 4, y: 8, z: 12 (z_hi: 4, z_lo: 3; z = z_hi * 3 + z_lo), core: 2. Of those that a mesh axis runs over, the one named last changes fastest.
Arguments:
- img_features: bfloat16 [1536, 256, 1024], P(('dp', 'neg'))
- txt_features: bfloat16 [1536, 64, 1024], P(('dp', 'neg'))
- w_img: bfloat16 [1024, 256], replicated
- w_txt: bfloat16 [1024, 256], replicated
- cap_len: int32 [1536], P(('dp', 'neg')), may hold values from 16 to 64
- pairs: int32 [64, 24], P('dp'), may hold values from 0 to 23, each once within a row
Outputs:
- grad_img_features: bfloat16 [1536, 256, 1024], P(('dp', 'neg'))
- grad_txt_features: bfloat16 [1536, 64, 1024], P(('dp', 'neg'))
- grad_w_img: float32 [1024, 256], P('dp')
- grad_w_txt: float32 [1024, 256], P('dp')
The draws below stay inside these ranges and needn't reach their ends.
Inputs may be any that keep to these rules, and one draw needn't show every extreme that they name: `pairs`: each row is a permutation of 0 to 23.
All inputs are finite; a program needn't handle non-finite values.
Results may differ from the reference program's by a relative error of at most 0.011.
Values may be sent and summed in bfloat16 or wider, within the bound.
No kernel may reach another device: no remote copies, remote signals or barrier semaphores. Data moves between devices by JAX's collectives and lax.ppermute only.
A program may use at most 64 MiB of HBM per device.

```python
import jax
import jax.numpy as jnp
from jax import lax

D_IN = 1024
EMB = 256
PI = 256
PT = 64
GROUP = 24
IMAGES = 1536
N_DP = 64


def shared_weight(key):
    return jax.random.normal(jax.random.fold_in(key, 11), (D_IN, EMB), jnp.float32) * D_IN ** (-0.5)


def group_common(key):
    common = jax.random.normal(jax.random.fold_in(key, 31), (N_DP, 1, 1, D_IN), jnp.float32)
    return jnp.broadcast_to(common, (N_DP, GROUP, 1, D_IN)).reshape(IMAGES, 1, D_IN)


def image_tokens(key, ramp):
    base = jax.random.normal(jax.random.fold_in(key, 21), (IMAGES, PI, D_IN), jnp.float32)
    place = (jnp.arange(IMAGES, dtype=jnp.int32) % GROUP).astype(jnp.float32)
    rising = ramp * place / max(GROUP - 1, 1)
    return base + rising[:, None, None] * group_common(key)


def draw_w_img(key, part):
    return shared_weight(key).astype(jnp.bfloat16)


def draw_w_txt(key, part):
    return (jax.random.normal(jax.random.fold_in(key, 12), (D_IN, EMB), jnp.float32) * D_IN ** (-0.5)).astype(jnp.bfloat16)


def draw_img_features(key, part):
    return image_tokens(key, 0.2).astype(jnp.bfloat16)


def draw_txt_features(key, part):
    common = group_common(key)
    fresh = jax.random.normal(jax.random.fold_in(key, 22), (IMAGES, PT, D_IN), jnp.float32)
    return (fresh + 0.3 * common).astype(jnp.bfloat16)


def touch_ends(drawn, own_key, smallest, high):
    spot = [jax.random.randint(jax.random.fold_in(own_key, axis), (), 0, length) for axis, length in enumerate(drawn.shape)]
    widest = drawn.shape.index(max(drawn.shape))
    next_to = spot[:widest] + [(spot[widest] + 1) % drawn.shape[widest]] + spot[widest + 1:]
    return drawn.at[tuple(spot)].set(smallest).at[tuple(next_to)].set(high)


def setup_inputs(seed: int = 0) -> dict:
    key_of = jax.random.split(jax.random.key(seed), 7)
    img_features = draw_img_features(jax.random.fold_in(key_of[6], 71), 0)
    txt_features = draw_txt_features(jax.random.fold_in(key_of[6], 71), 0)
    w_img = draw_w_img(jax.random.fold_in(key_of[6], 71), 0)
    w_txt = draw_w_txt(jax.random.fold_in(key_of[6], 71), 0)
    cap_len = touch_ends(jax.random.randint(key_of[4], (IMAGES,), PT // 4, PT + 1), jax.random.fold_in(key_of[4], 1), PT // 4, PT).astype(jnp.int32)
    pairs = jax.vmap(lambda own: jax.random.permutation(own, GROUP))(jax.random.split(key_of[5], N_DP)).reshape((N_DP, GROUP)).astype(jnp.int32)
    return {"img_features": img_features, "txt_features": txt_features, "w_img": w_img, "w_txt": w_txt, "cap_len": cap_len, "pairs": pairs}


TOKEN_SCALE = 100.0
PAIR_SCALE = 50.0
EPSILON = 1e-06

def unit_rows(projected):
    inverse = lax.rsqrt(lax.optimization_barrier(jnp.sum(projected * projected, axis=-1, keepdims=True)) + EPSILON)
    return (projected * inverse, inverse)

def back_unit(gradient, unit, inverse):
    return (gradient - unit * lax.optimization_barrier(jnp.sum(unit * gradient, axis=-1, keepdims=True))) * inverse

def token_pool(scores, lengths, count_caps, text_len):
    rows = scores.shape[0]
    logits = (TOKEN_SCALE * scores).reshape(rows, count_caps, text_len)
    valid = (jnp.arange(text_len, dtype=jnp.int32)[None, :] < lengths[:, None])[None]
    peaks = lax.optimization_barrier(jnp.max(jnp.where(valid, logits, -jnp.inf), axis=2, keepdims=True))
    expos = jnp.where(valid, jnp.exp(logits - peaks), 0.0)
    totals = lax.optimization_barrier(jnp.sum(expos, axis=2, keepdims=True))
    pooled = (peaks[..., 0] + jnp.log(totals[..., 0])) / TOKEN_SCALE
    return (pooled, expos / totals)

def group_grads(img, txt, lengths, perm, w_img, w_txt):
    count = img.shape[0]
    img_len = img.shape[1]
    text_len = txt.shape[1]
    img_flat = img.reshape(count * img_len, img.shape[2])
    txt_flat = txt.reshape(count * text_len, txt.shape[2])
    img_unit, img_inv = unit_rows(jnp.dot(img_flat, w_img, preferred_element_type=jnp.float32))
    txt_unit, txt_inv = unit_rows(jnp.dot(txt_flat, w_txt, preferred_element_type=jnp.float32))
    img_half = img_unit.astype(jnp.bfloat16)
    txt_half = txt_unit.astype(jnp.bfloat16)
    scores = jnp.dot(img_half, txt_half.T, preferred_element_type=jnp.float32)
    pooled, weights = token_pool(scores, lengths, count, text_len)
    logits = PAIR_SCALE * lax.optimization_barrier(jnp.mean(pooled.reshape(count, img_len, count), axis=1))
    target = (perm[:, None] == jnp.arange(count, dtype=jnp.int32)[None, :]).astype(jnp.float32)
    row_prob = jax.nn.softmax(logits, axis=1)
    col_prob = jax.nn.softmax(logits, axis=0)
    pair_grad = (row_prob + col_prob - 2.0 * target) * (PAIR_SCALE / (2.0 * count * img_len))
    spread = jnp.broadcast_to(pair_grad[:, None, :], (count, img_len, count)).reshape(count * img_len, count, 1)
    score_grad = (spread * weights).reshape(count * img_len, count * text_len).astype(jnp.bfloat16)
    img_grad = jnp.dot(score_grad, txt_half, preferred_element_type=jnp.float32)
    txt_grad = jnp.dot(score_grad.T, img_half, preferred_element_type=jnp.float32)
    img_back = back_unit(img_grad, img_unit, img_inv).astype(jnp.bfloat16)
    txt_back = back_unit(txt_grad, txt_unit, txt_inv).astype(jnp.bfloat16)
    feat_img = jnp.dot(img_back, w_img.T, preferred_element_type=jnp.float32).astype(jnp.bfloat16)
    feat_txt = jnp.dot(txt_back, w_txt.T, preferred_element_type=jnp.float32).astype(jnp.bfloat16)
    wgrad_img = jnp.dot(img_flat.T, img_back, preferred_element_type=jnp.float32)
    wgrad_txt = jnp.dot(txt_flat.T, txt_back, preferred_element_type=jnp.float32)
    return (feat_img.reshape(img.shape), feat_txt.reshape(txt.shape), wgrad_img, wgrad_txt)

def reference(img_features, txt_features, w_img, w_txt, cap_len, pairs):
    img_groups = img_features.reshape(N_DP, GROUP, PI, D_IN)
    txt_groups = txt_features.reshape(N_DP, GROUP, PT, D_IN)
    len_groups = cap_len.reshape(N_DP, GROUP)

    def one_group(packed):
        return group_grads(packed[0], packed[1], packed[2], packed[3], w_img, w_txt)
    feat_img, feat_txt, wgrad_img, wgrad_txt = lax.map(one_group, (img_groups, txt_groups, len_groups, pairs))
    return (feat_img.reshape(IMAGES, PI, D_IN), feat_txt.reshape(IMAGES, PT, D_IN), lax.optimization_barrier(jnp.sum(wgrad_img, axis=0)), lax.optimization_barrier(jnp.sum(wgrad_txt, axis=0)))
```

```python
import jax
import jax.numpy as jnp
from jax import lax
from jax.experimental import pallas as pl
from jax.experimental.pallas import tpu as pltpu
from jax.sharding import Mesh
from jax.sharding import PartitionSpec as P

NEG = ("neg_0", "neg_1")
DP_NEG = ("dp", "neg_0", "neg_1")

TOKEN_SCALE = 100.0
PAIR_SCALE = 50.0
EPSILON = 1e-06
LOG2E = 1.4426950408889634
LOW = -1e30
F32 = jnp.float32
BF16 = jnp.bfloat16

VMEM = pl.BlockSpec(memory_space=pltpu.VMEM)
SMEM = pl.BlockSpec(memory_space=pltpu.SMEM)


def call(kernel, outs, specs, flops, scratch=()):
    moved = sum(o.size * o.dtype.itemsize for o in outs)
    return pl.pallas_call(
        kernel,
        out_shape=tuple(outs),
        in_specs=specs,
        out_specs=tuple(VMEM for _ in outs),
        scratch_shapes=list(scratch),
        cost_estimate=pl.CostEstimate(flops=flops, bytes_accessed=2 * moved, transcendentals=0),
    )


def shape(dims, dtype):
    return jax.ShapeDtypeStruct(dims, dtype)


def along_rows(a, b):
    return lax.dot_general(a, b, (((0,), (0,)), ((), ())), preferred_element_type=F32)


def along_last(a, b):
    return lax.dot_general(a, b, (((1,), (1,)), ((), ())), preferred_element_type=F32)


def unit_rows(projected):
    inverse = lax.rsqrt(jnp.sum(projected * projected, axis=-1, keepdims=True) + EPSILON)
    return (projected * inverse, inverse)


def back_unit(gradient, unit, inverse):
    return (gradient - unit * jnp.sum(unit * gradient, axis=-1, keepdims=True)) * inverse


def text_kernel(len_ref, x_ref, w_ref, out_ref, unit_ref, inv_ref):
    unit, inverse = unit_rows(jnp.dot(x_ref[...], w_ref[...], preferred_element_type=F32))
    unit_ref[...] = unit
    inv_ref[...] = jnp.broadcast_to(inverse, inv_ref.shape)
    half = unit.astype(BF16)
    rows = half.shape[0]
    line = lax.broadcasted_iota(jnp.int32, (8, half.shape[1]), 0)
    lens = jnp.where(line == 0, len_ref[0], len_ref[1]).astype(F32).astype(BF16)
    for d in range(out_ref.shape[0]):
        out_ref[d, :rows, :] = half
        out_ref[d, rows:, :] = lens


def image_kernel(x_ref, w_ref, unit_ref, inv_ref, half_ref):
    unit, inverse = unit_rows(jnp.dot(x_ref[...], w_ref[...], preferred_element_type=F32))
    unit_ref[...] = unit
    inv_ref[...] = jnp.broadcast_to(inverse, inv_ref.shape)
    half_ref[...] = unit.astype(BF16)


def score_kernel(text_len, img_len, g_ref, half_ref, wt_ref, stats_ref, pooled_ref):
    owners = g_ref.shape[0]
    rows = 2 * text_len
    columns = half_ref.shape[0]
    half = half_ref[...]
    token = lax.broadcasted_iota(jnp.int32, (text_len, 128), 0).astype(F32)
    pooled_ref[...] = jnp.zeros_like(pooled_ref)
    for d in range(owners):
        scores = along_last(g_ref[d, :rows, :], half)
        lens = g_ref[d, rows:, :128].astype(F32)
        for j in range(2):
            keep = token < lens[j : j + 1, :]
            keep = jnp.concatenate([keep] * (columns // 128), axis=1)
            own = jnp.where(keep, scores[j * text_len : (j + 1) * text_len], LOW)
            top = jnp.max(own, axis=0, keepdims=True)
            expos = jnp.exp2((own - top) * (TOKEN_SCALE * LOG2E))
            total = jnp.sum(expos, axis=0, keepdims=True)
            b = 2 * d + j
            wt_ref[b * text_len : (b + 1) * text_len, :] = (expos * (1.0 / total)).astype(BF16)
            pooled_ref[b : b + 1, :] = top + jnp.log(total) / TOKEN_SCALE
    lane = lax.broadcasted_iota(jnp.int32, (128, 128), 1)
    first = jnp.sum(pooled_ref[:, :img_len], axis=1, keepdims=True)
    second = jnp.sum(pooled_ref[:, img_len:], axis=1, keepdims=True)
    table = jnp.where(lane == 0, first, second) * (PAIR_SCALE / img_len)
    logits = table.T[:8, :]
    line = lax.broadcasted_iota(jnp.int32, logits.shape, 0)
    logits = jnp.where(line < 2, logits, LOW)
    for d in range(owners):
        stats_ref[d] = logits


def terms_kernel(wt_ref, half_ref, terms_ref):
    img_len = half_ref.shape[0] // 2
    for a in range(2):
        part = slice(a * img_len, (a + 1) * img_len)
        terms_ref[a] = jnp.dot(wt_ref[:, part], half_ref[part, :], preferred_element_type=F32)


def pair_kernel(group_size, img_len, perm_ref, all_ref, own_ref, terms_ref, pay_ref, pair_ref):
    owners = all_ref.shape[0]
    text_len = pay_ref.shape[1] // 2
    everyone = all_ref[...].reshape(owners * 8, 128)
    col_top = jnp.max(everyone, axis=0, keepdims=True)
    col_sum = jnp.sum(jnp.exp(everyone - col_top), axis=0, keepdims=True)
    own = own_ref[0]
    lane = lax.broadcasted_iota(jnp.int32, own.shape, 1)
    line = lax.broadcasted_iota(jnp.int32, own.shape, 0)
    row = jnp.where(lane < group_size, own, LOW)
    expos = jnp.exp(row - jnp.max(row, axis=1, keepdims=True))
    row_prob = expos / jnp.sum(expos, axis=1, keepdims=True)
    col_prob = jnp.exp(own - col_top) / col_sum
    target = (lane == jnp.where(line == 0, perm_ref[0], perm_ref[1])).astype(F32)
    pair = (row_prob + col_prob - 2.0 * target) * (PAIR_SCALE / (2.0 * group_size * img_len))
    pair = jnp.concatenate([pair, jnp.zeros((120, 128), F32)], axis=0).T
    pair_ref[...] = pair
    for b in range(2 * owners):
        part = slice(b * text_len, (b + 1) * text_len)
        both = terms_ref[0, part, :] * pair[b : b + 1, 0:1] + terms_ref[1, part, :] * pair[b : b + 1, 1:2]
        pay_ref[b // 2, (b % 2) * text_len : (b % 2 + 1) * text_len, :] = both.astype(BF16)


def put_pieces(out_ref, grads):
    tiles = grads.reshape(-1, 16, grads.shape[1])
    for j in range(4):
        h, k = j // 2, j % 2
        piece = tiles[:, 8 * h : 8 * h + 8, 128 * k : 128 * k + 128]
        out_ref[j] = piece.reshape(out_ref.shape[1:]).astype(BF16)


def image_back_kernel(text_len, pair_ref, g_ref, wt_ref, unit_ref, inv_ref, x_ref, back_ref, pay_ref, scaled_ref):
    owners = g_ref.shape[0]
    img_len = unit_ref.shape[0] // 2
    for a in range(2):
        for b in range(2 * owners):
            text = g_ref[b // 2, (b % 2) * text_len : (b % 2 + 1) * text_len, :].astype(F32)
            scaled = text * pair_ref[b : b + 1, a : a + 1]
            scaled_ref[b * text_len : (b + 1) * text_len, :] = scaled.astype(BF16)
        part = slice(a * img_len, (a + 1) * img_len)
        gradient = along_rows(wt_ref[:, part], scaled_ref[...])
        back = back_unit(gradient, unit_ref[part, :], inv_ref[part, :1])
        back_ref[part, :] = back.astype(BF16)
    put_pieces(pay_ref, along_rows(x_ref[...], back_ref[...]))


def text_back_kernel(all_ref, unit_ref, inv_ref, x_ref, back_ref, pay_ref):
    gradient = all_ref[0].astype(F32)
    for d in range(1, all_ref.shape[0]):
        gradient += all_ref[d].astype(F32)
    back = back_unit(gradient, unit_ref[...], inv_ref[:, :1]).astype(BF16)
    back_ref[...] = back
    put_pieces(pay_ref, along_rows(x_ref[...], back))


def partial_kernel(all_ref, out_ref):
    total = all_ref[0].astype(F32)
    for d in range(1, all_ref.shape[0]):
        total += all_ref[d].astype(F32)
    out_ref[...] = total.astype(BF16).reshape(out_ref.shape)


def rows_kernel(img_ref, txt_ref, out_ref):
    img = jnp.sum(img_ref[...].astype(F32), axis=0)
    txt = jnp.sum(txt_ref[...].astype(F32), axis=0)
    for d in range(out_ref.shape[0]):
        out_ref[d, :8, :] = img
        out_ref[d, 8:, :] = txt


def final_kernel(outer, all_ref, img_ref, txt_ref):
    inner = all_ref.shape[0] // outer
    for j in range(inner):
        total = all_ref[j]
        for i in range(1, outer):
            total += all_ref[i * inner + j]
        h, k = j // 2, j % 2
        img_ref[8 * h : 8 * h + 8, 128 * k : 128 * k + 128] = total[:8]
        txt_ref[8 * h : 8 * h + 8, 128 * k : 128 * k + 128] = total[8:]


def swap(array, axis):
    return lax.all_to_all(array, axis, 0, 0, tiled=True)


def shards(img_features, txt_features, w_img, w_txt, cap_len, pairs):
    local_count, img_len, depth = img_features.shape
    text_len = txt_features.shape[1]
    width = w_img.shape[1]
    owners = lax.axis_size(NEG)
    outer = lax.axis_size("neg_0")
    dp = lax.axis_size("dp")
    group_size = owners * local_count
    img_rows, txt_rows = local_count * img_len, local_count * text_len
    img_flat = img_features.reshape(img_rows, depth)
    txt_flat = txt_features.reshape(txt_rows, depth)
    start = lax.axis_index(NEG) * local_count
    perm = lax.dynamic_slice_in_dim(pairs[0], start, local_count)

    sent, txt_unit, txt_inv = call(
        text_kernel,
        [shape((owners, txt_rows + 8, width), BF16), shape((txt_rows, width), F32), shape((txt_rows, 128), F32)],
        [SMEM, VMEM, VMEM],
        2 * txt_rows * depth * width,
    )(cap_len, txt_flat, w_txt)
    group = swap(sent, NEG)
    img_unit, img_inv, img_half = call(
        image_kernel,
        [shape((img_rows, width), F32), shape((img_rows, 128), F32), shape((img_rows, width), BF16)],
        [VMEM, VMEM],
        2 * img_rows * depth * width,
    )(img_flat, w_img)
    weights, own = call(
        lambda *refs: score_kernel(text_len, img_len, *refs),
        [shape((group_size * text_len, img_rows), BF16), shape((owners, 8, 128), F32)],
        [VMEM, VMEM],
        2 * group_size * text_len * img_rows * width,
        [pltpu.VMEM((128, img_rows), F32)],
    )(group, img_half)
    everyone = swap(own, NEG)
    (terms,) = call(
        terms_kernel,
        [shape((local_count, group_size * text_len, width), F32)],
        [VMEM, VMEM],
        2 * group_size * text_len * img_rows * width,
    )(weights, img_half)
    text_terms, pair = call(
        lambda *refs: pair_kernel(group_size, img_len, *refs),
        [shape((owners, txt_rows, width), BF16), shape((128, 128), F32)],
        [SMEM, VMEM, VMEM, VMEM],
        4 * group_size * text_len * width,
    )(perm, everyone, own, terms)
    arrived = swap(text_terms, NEG)
    img_back, img_pieces = call(
        lambda *refs: image_back_kernel(text_len, *refs),
        [shape((img_rows, width), BF16), shape((4, depth // 2, 128), BF16)],
        [VMEM] * 6,
        2 * img_rows * width * (group_size * text_len + depth),
        [pltpu.VMEM((group_size * text_len, width), BF16)],
    )(pair, group, weights, img_unit, img_inv, img_flat)
    img_quarter = swap(img_pieces, "neg_1")
    txt_back, txt_pieces = call(
        text_back_kernel,
        [shape((txt_rows, width), BF16), shape((4, depth // 2, 128), BF16)],
        [VMEM] * 4,
        2 * txt_rows * width * depth,
    )(arrived, txt_unit, txt_inv, txt_flat)
    txt_quarter = swap(txt_pieces, "neg_1")
    partial = lambda quarter: call(
        partial_kernel, [shape((dp, 8, 128), BF16)], [VMEM], 4 * depth * 64
    )(quarter)[0]
    img_rows_all = swap(partial(img_quarter), "dp")
    txt_rows_all = swap(partial(txt_quarter), "dp")
    (mine,) = call(
        rows_kernel, [shape((owners, 16, 128), F32)], [VMEM, VMEM], 2 * dp * 1024
    )(img_rows_all, txt_rows_all)
    final_img, final_txt = call(
        lambda *refs: final_kernel(outer, *refs),
        [shape((16, width), F32), shape((16, width), F32)],
        [VMEM],
        owners * 2048,
    )(swap(mine, NEG))
    feat_img = jnp.dot(img_back, w_img.T, preferred_element_type=F32).astype(BF16)
    feat_txt = jnp.dot(txt_back, w_txt.T, preferred_element_type=F32).astype(BF16)
    return (
        feat_img.reshape(img_features.shape),
        feat_txt.reshape(txt_features.shape),
        final_img,
        final_txt,
    )


def solution(mesh):
    split = Mesh(mesh.devices.reshape(mesh.shape["dp"], 3, 4), ("dp", "neg_0", "neg_1"))
    return jax.shard_map(
        shards,
        mesh=split,
        in_specs=(P(DP_NEG, None, None), P(DP_NEG, None, None), P(), P(), P(DP_NEG), P("dp", None)),
        out_specs=(P(DP_NEG, None, None), P(DP_NEG, None, None), P("dp", None), P("dp", None)),
        check_vma=False,
    )
```

```python
import jax
import jax.numpy as jnp
from jax import lax
from jax.experimental import pallas as pl
from jax.experimental.pallas import tpu as pltpu
from jax.sharding import Mesh
from jax.sharding import PartitionSpec as P

NEG = ("neg_0", "neg_1")
DP_NEG = ("dp", "neg_0", "neg_1")

TOKEN_SCALE = 100.0
PAIR_SCALE = 50.0
EPSILON = 1e-06
LOG2E = 1.4426950408889634
LOW = -1e30
SCORE_GRANT = 52
PAIR_GRANT = 52
BACK_GRANT = 53
F32 = jnp.float32
BF16 = jnp.bfloat16

VMEM = pl.BlockSpec(memory_space=pltpu.VMEM)
SMEM = pl.BlockSpec(memory_space=pltpu.SMEM)
HBM = pl.BlockSpec(memory_space=pltpu.HBM)


def call(kernel, outs, specs, flops, scratch=(), grant=8, places=None):
    moved = sum(o.size * o.dtype.itemsize for o in outs)
    return pl.pallas_call(
        kernel,
        out_shape=tuple(outs),
        in_specs=specs,
        out_specs=tuple(places or [VMEM] * len(outs)),
        scratch_shapes=list(scratch),
        cost_estimate=pl.CostEstimate(flops=flops, bytes_accessed=2 * moved, transcendentals=0),
        compiler_params=pltpu.CompilerParams(vmem_limit_bytes=int(grant * 2**20)),
    )


def shape(dims, dtype):
    return jax.ShapeDtypeStruct(dims, dtype)


def along_rows(a, b):
    return lax.dot_general(a, b, (((0,), (0,)), ((), ())), preferred_element_type=F32)


def along_last(a, b):
    return lax.dot_general(a, b, (((1,), (1,)), ((), ())), preferred_element_type=F32)


def unit_rows(projected):
    inverse = lax.rsqrt(jnp.sum(projected * projected, axis=-1, keepdims=True) + EPSILON)
    return (projected * inverse, inverse)


def back_unit(gradient, unit, inverse):
    return (gradient - unit * jnp.sum(unit * gradient, axis=-1, keepdims=True)) * inverse


def copy(source, target, sem):
    moving = pltpu.make_async_copy(source, target, sem)
    moving.start()
    return moving


def text_kernel(len_ref, x_ref, w_ref, out_ref):
    unit, _ = unit_rows(jnp.dot(x_ref[...], w_ref[...], preferred_element_type=F32))
    half = unit.astype(BF16)
    rows, width = half.shape
    line = lax.broadcasted_iota(jnp.int32, (8, width), 0)
    lens = jnp.where(line == 0, len_ref[0], len_ref[1]).astype(F32).astype(BF16)
    for d in range(out_ref.shape[0]):
        out_ref[d, :rows, :] = half
        out_ref[d, rows:, :] = lens


def unit_kernel(x_ref, w_ref, unit_ref, inv_ref):
    unit, inverse = unit_rows(jnp.dot(x_ref[...], w_ref[...], preferred_element_type=F32))
    unit_ref[...] = unit
    inv_ref[...] = jnp.broadcast_to(inverse, inv_ref.shape)


def image_kernel(x_ref, w_ref, half_ref):
    unit, _ = unit_rows(jnp.dot(x_ref[...], w_ref[...], preferred_element_type=F32))
    half_ref[...] = unit.astype(BF16)


def score_kernel(text_len, img_len, g_ref, half_ref, wt_hbm, stats_hbm, wt_ref, pooled_ref, logits_ref, wt_sem, sem):
    owners = g_ref.shape[0]
    rows = 2 * text_len
    columns = half_ref.shape[0]
    half = half_ref[...]
    token = lax.broadcasted_iota(jnp.int32, (text_len, 128), 0).astype(F32)
    pooled_ref[...] = jnp.zeros_like(pooled_ref)
    moving = []
    for d in range(owners):
        scores = along_last(g_ref[d, :rows, :], half)
        lens = g_ref[d, rows:, :128].astype(F32)
        for j in range(2):
            keep = token < lens[j : j + 1, :]
            keep = jnp.concatenate([keep] * (columns // 128), axis=1)
            own = jnp.where(keep, scores[j * text_len : (j + 1) * text_len], LOW)
            top = jnp.max(own, axis=0, keepdims=True)
            expos = jnp.exp2((own - top) * (TOKEN_SCALE * LOG2E))
            total = jnp.sum(expos, axis=0, keepdims=True)
            b = 2 * d + j
            wt_ref[b * text_len : (b + 1) * text_len, :] = (expos * (1.0 / total)).astype(BF16)
            pooled_ref[b : b + 1, :] = top + jnp.log(total) / TOKEN_SCALE
        part = pl.ds(d * rows, rows)
        moving.append(copy(wt_ref.at[part, :], wt_hbm.at[part, :], wt_sem.at[d]))
    lane = lax.broadcasted_iota(jnp.int32, (128, 128), 1)
    first = jnp.sum(pooled_ref[:, :img_len], axis=1, keepdims=True)
    second = jnp.sum(pooled_ref[:, img_len:], axis=1, keepdims=True)
    table = jnp.where(lane == 0, first, second) * (PAIR_SCALE / img_len)
    logits = table.T[:8, :]
    line = lax.broadcasted_iota(jnp.int32, logits.shape, 0)
    logits_ref[...] = jnp.where(line < 2, logits, LOW)
    moving += [copy(logits_ref, stats_hbm.at[d], sem.at[d]) for d in range(owners)]
    for one in moving:
        one.wait()


def pair_kernel(
    group_size, img_len, pairs_ref, all_ref, own_ref, half_ref, wt_hbm, pay_hbm, pair_hbm,
    wt_ref, terms_ref, pair_ref, pay_ref, wt_sem, pair_sem, sem,
):
    owners = all_ref.shape[0]
    text_len = pay_ref.shape[1] // 2
    weights = copy(wt_hbm, wt_ref, wt_sem)
    start = (lax.axis_index("neg_0") * lax.axis_size("neg_1") + lax.axis_index("neg_1")) * 2
    everyone = all_ref[...].reshape(owners * 8, 128)
    col_top = jnp.max(everyone, axis=0, keepdims=True)
    col_sum = jnp.sum(jnp.exp(everyone - col_top), axis=0, keepdims=True)
    own = own_ref[0]
    lane = lax.broadcasted_iota(jnp.int32, own.shape, 1)
    line = lax.broadcasted_iota(jnp.int32, own.shape, 0)
    row = jnp.where(lane < group_size, own, LOW)
    expos = jnp.exp(row - jnp.max(row, axis=1, keepdims=True))
    row_prob = expos / jnp.sum(expos, axis=1, keepdims=True)
    col_prob = jnp.exp(own - col_top) / col_sum
    target = (lane == jnp.where(line == 0, pairs_ref[0, start], pairs_ref[0, start + 1])).astype(F32)
    pair = (row_prob + col_prob - 2.0 * target) * (PAIR_SCALE / (2.0 * group_size * img_len))
    pair = jnp.concatenate([pair, jnp.zeros((120, 128), F32)], axis=0).T
    pair_ref[...] = pair
    moving = [copy(pair_ref, pair_hbm.at[0], pair_sem)]
    weights.wait()
    for a in range(2):
        part = slice(a * img_len, (a + 1) * img_len)
        terms_ref[a] = jnp.dot(wt_ref[:, part], half_ref[part, :], preferred_element_type=F32)
    for d in range(owners):
        for j in range(2):
            b = 2 * d + j
            part = slice(b * text_len, (b + 1) * text_len)
            both = terms_ref[0, part, :] * pair[b : b + 1, 0:1] + terms_ref[1, part, :] * pair[b : b + 1, 1:2]
            pay_ref[d, j * text_len : (j + 1) * text_len, :] = both.astype(BF16)
        moving.append(copy(pay_ref.at[d], pay_hbm.at[d], sem.at[d]))
    for one in moving:
        one.wait()


def image_back_kernel(
    text_len, pair_hbm, g_hbm, wt_hbm, w_hbm, x_hbm, back_hbm, *refs
):
    turned, refs = refs[:4], refs[4:]
    pair_ref, g_ref, wt_ref, w_ref, x_ref, scaled_ref, back_ref, pay_ref, in_sem, out_sem = refs
    owners = g_ref.shape[0]
    pair = copy(pair_hbm.at[0], pair_ref, in_sem.at[4])
    group = copy(g_hbm, g_ref, in_sem.at[0])
    image = copy(x_hbm, x_ref, in_sem.at[1])
    projection = copy(w_hbm, w_ref, in_sem.at[2])
    weights = copy(wt_hbm, wt_ref, in_sem.at[3])
    img_len = x_ref.shape[0] // 2
    pair.wait()
    group.wait()
    for a in range(2):
        for b in range(2 * owners):
            text = g_ref[b // 2, (b % 2) * text_len : (b % 2 + 1) * text_len, :].astype(F32)
            scaled = text * pair_ref[b : b + 1, a : a + 1]
            scaled_ref[a, b * text_len : (b + 1) * text_len, :] = scaled.astype(BF16)
    image.wait()
    projection.wait()
    unit, inverse = unit_rows(jnp.dot(x_ref[...], w_ref[...], preferred_element_type=F32))
    weights.wait()
    for a in range(2):
        part = slice(a * img_len, (a + 1) * img_len)
        gradient = along_rows(wt_ref[:, part], scaled_ref[a])
        back_ref[part, :] = back_unit(gradient, unit[part], inverse[part]).astype(BF16)
    result = copy(back_ref, back_hbm, out_sem.at[4])
    tiles = along_rows(x_ref[...], back_ref[...]).reshape(-1, 16, back_ref.shape[1])
    for j in range(4):
        h, k = j // 2, j % 2
        piece = tiles[:, 8 * h : 8 * h + 8, 128 * k : 128 * k + 128]
        pay_ref[j] = piece.reshape(pay_ref.shape[1:]).astype(BF16)
    me = lax.axis_index("neg_1")
    moving = [
        copy(pay_ref.at[lax.rem(me + turn, 4)], target, out_sem.at[turn]) for turn, target in enumerate(turned)
    ]
    for one in moving:
        one.wait()
    result.wait()


def text_back_kernel(all_ref, unit_ref, inv_ref, x_ref, back_ref, pay_ref):
    gradient = all_ref[0].astype(F32)
    for d in range(1, all_ref.shape[0]):
        gradient += all_ref[d].astype(F32)
    back = back_unit(gradient, unit_ref[...], inv_ref[:, :1]).astype(BF16)
    back_ref[...] = back
    tiles = along_rows(x_ref[...], back).reshape(-1, 16, back.shape[1])
    for j in range(4):
        h, k = j // 2, j % 2
        piece = tiles[:, 8 * h : 8 * h + 8, 128 * k : 128 * k + 128]
        pay_ref[j] = piece.reshape(pay_ref.shape[1:]).astype(BF16)


def partial_kernel(*refs):
    images, txt_ref, out_ref = refs[:-2], refs[-2], refs[-1]
    groups = ([r[...] for r in images], [txt_ref[d] for d in range(txt_ref.shape[0])])
    for k, parts in enumerate(groups):
        total = parts[0].astype(F32)
        for part in parts[1:]:
            total += part.astype(F32)
        out_ref[:, 8 * k : 8 * k + 8, :] = total.astype(BF16).reshape(out_ref.shape[0], 8, 128)


def rows_kernel(all_ref, out_ref):
    total = jnp.sum(all_ref[...].astype(F32), axis=0)
    for d in range(out_ref.shape[0]):
        out_ref[d] = total


def final_kernel(outer, all_ref, img_ref, txt_ref):
    inner = all_ref.shape[0] // outer
    for j in range(inner):
        total = all_ref[j]
        for i in range(1, outer):
            total += all_ref[i * inner + j]
        h, k = j // 2, j % 2
        img_ref[8 * h : 8 * h + 8, 128 * k : 128 * k + 128] = total[:8]
        txt_ref[8 * h : 8 * h + 8, 128 * k : 128 * k + 128] = total[8:]


def swap(array, axis):
    return lax.all_to_all(array, axis, 0, 0, tiled=True)


def window(img_features, txt_features, w_img, w_txt, cap_len, pairs):
    local_count, img_len, depth = img_features.shape
    text_len = txt_features.shape[1]
    width = w_img.shape[1]
    owners = lax.axis_size(NEG)
    outer = lax.axis_size("neg_0")
    dp = lax.axis_size("dp")
    group_size = owners * local_count
    img_rows, txt_rows = local_count * img_len, local_count * text_len
    img_flat = img_features.reshape(img_rows, depth)
    txt_flat = txt_features.reshape(txt_rows, depth)
    DMA = pltpu.SemaphoreType.DMA

    (sent,) = call(
        text_kernel,
        [shape((owners, txt_rows + 8, width), BF16)],
        [SMEM, VMEM, VMEM],
        2 * txt_rows * depth * width,
        grant=63,
    )(cap_len, txt_flat, w_txt)
    group = swap(sent, NEG)
    (img_half,) = call(
        image_kernel, [shape((img_rows, width), BF16)], [VMEM, VMEM], 2 * img_rows * depth * width
    )(img_flat, w_img)
    weights, own = call(
        lambda *refs: score_kernel(text_len, img_len, *refs),
        [shape((group_size * text_len, img_rows), BF16), shape((owners, 8, 128), F32)],
        [VMEM, VMEM],
        2 * group_size * text_len * img_rows * width,
        [
            pltpu.VMEM((group_size * text_len, img_rows), BF16),
            pltpu.VMEM((128, img_rows), F32),
            pltpu.VMEM((8, 128), F32),
            DMA((owners,)),
            DMA((owners,)),
        ],
        places=[HBM, HBM],
        grant=SCORE_GRANT,
    )(group, img_half)
    everyone = swap(own, NEG)
    text_terms, pair = call(
        lambda *refs: pair_kernel(group_size, img_len, *refs),
        [shape((owners, txt_rows, width), BF16), shape((32, 128, 128), F32)],
        [SMEM, VMEM, VMEM, VMEM, HBM],
        2 * group_size * text_len * img_rows * width,
        [
            pltpu.VMEM((group_size * text_len, img_rows), BF16),
            pltpu.VMEM((local_count, group_size * text_len, width), F32),
            pltpu.VMEM((128, 128), F32),
            pltpu.VMEM((owners, txt_rows, width), BF16),
            DMA,
            DMA,
            DMA((owners,)),
        ],
        places=[HBM, HBM],
        grant=PAIR_GRANT,
    )(pairs, everyone, own, img_half, weights)
    arrived = swap(text_terms, NEG)
    img_back, *turned = call(
        lambda *refs: image_back_kernel(text_len, *refs),
        [shape((img_rows, width), BF16)] + [shape((depth // 2, 128), BF16)] * 4,
        [HBM, HBM, HBM, HBM, HBM],
        2 * img_rows * width * (group_size * text_len + depth),
        [
            pltpu.VMEM((128, 128), F32),
            pltpu.VMEM((owners, txt_rows + 8, width), BF16),
            pltpu.VMEM((group_size * text_len, img_rows), BF16),
            pltpu.VMEM((depth, width), BF16),
            pltpu.VMEM((img_rows, depth), BF16),
            pltpu.VMEM((2, group_size * text_len, width), BF16),
            pltpu.VMEM((img_rows, width), BF16),
            pltpu.VMEM((4, depth // 2, 128), BF16),
            DMA((5,)),
            DMA((5,)),
        ],
        places=[HBM] * 5,
        grant=BACK_GRANT,
    )(pair, group, weights, w_img, img_flat)
    for turn in range(1, 4):
        turned[turn] = lax.ppermute(turned[turn], "neg_1", [(k, (k + turn) % 4) for k in range(4)])
    txt_unit, txt_inv = call(
        unit_kernel,
        [shape((txt_rows, width), F32), shape((txt_rows, 128), F32)],
        [VMEM, VMEM],
        2 * txt_rows * width * depth,
    )(txt_flat, w_txt)
    txt_back, txt_pieces = call(
        text_back_kernel,
        [shape((txt_rows, width), BF16), shape((4, depth // 2, 128), BF16)],
        [VMEM] * 4,
        2 * txt_rows * width * depth,
    )(arrived, txt_unit, txt_inv, txt_flat)
    txt_quarter = swap(txt_pieces, "neg_1")
    (partial,) = call(partial_kernel, [shape((dp, 16, 128), BF16)], [VMEM] * 5, 8 * depth * 64)(
        *turned, txt_quarter
    )
    (mine,) = call(rows_kernel, [shape((owners, 16, 128), F32)], [VMEM], 2 * dp * 2048)(swap(partial, "dp"))
    final_img, final_txt = call(
        lambda *refs: final_kernel(outer, *refs),
        [shape((16, width), F32), shape((16, width), F32)],
        [VMEM],
        owners * 2048,
    )(swap(mine, NEG))
    feat_img = jnp.dot(img_back, w_img.T, preferred_element_type=F32).astype(BF16)
    feat_txt = jnp.dot(txt_back, w_txt.T, preferred_element_type=F32).astype(BF16)
    return (
        feat_img.reshape(img_features.shape),
        feat_txt.reshape(txt_features.shape),
        final_img,
        final_txt,
    )


def solution(mesh):
    split = Mesh(mesh.devices.reshape(mesh.shape["dp"], 3, 4), ("dp", "neg_0", "neg_1"))
    return jax.shard_map(
        window,
        mesh=split,
        in_specs=(P(DP_NEG, None, None), P(DP_NEG, None, None), P(), P(), P(DP_NEG), P("dp", None)),
        out_specs=(P(DP_NEG, None, None), P(DP_NEG, None, None), P("dp", None), P("dp", None)),
        check_vma=False,
    )
```

```python
import jax
import jax.numpy as jnp
from jax import lax
from jax.experimental import pallas as pl
from jax.experimental.pallas import tpu as pltpu
from jax.sharding import Mesh
from jax.sharding import PartitionSpec as P

NEG = ("neg_0", "neg_1")
DP_NEG = ("dp", "neg_0", "neg_1")

TOKEN_SCALE = 100.0
PAIR_SCALE = 50.0
EPSILON = 1e-06
LOG2E = 1.4426950408889634
LOW = -1e30
SCORE_GRANT = 52
PAIR_GRANT = 52
BACK_GRANT = 53
FEATURE_GRANT = 53
F32 = jnp.float32
BF16 = jnp.bfloat16

VMEM = pl.BlockSpec(memory_space=pltpu.VMEM)
SMEM = pl.BlockSpec(memory_space=pltpu.SMEM)
HBM = pl.BlockSpec(memory_space=pltpu.HBM)


def call(kernel, outs, specs, flops, scratch=(), grant=8, places=None):
    moved = sum(o.size * o.dtype.itemsize for o in outs)
    return pl.pallas_call(
        kernel,
        out_shape=tuple(outs),
        in_specs=specs,
        out_specs=tuple(places or [VMEM] * len(outs)),
        scratch_shapes=list(scratch),
        cost_estimate=pl.CostEstimate(flops=flops, bytes_accessed=2 * moved, transcendentals=0),
        compiler_params=pltpu.CompilerParams(vmem_limit_bytes=int(grant * 2**20)),
    )


def shape(dims, dtype):
    return jax.ShapeDtypeStruct(dims, dtype)


def along_rows(a, b):
    return lax.dot_general(a, b, (((0,), (0,)), ((), ())), preferred_element_type=F32)


def along_last(a, b):
    return lax.dot_general(a, b, (((1,), (1,)), ((), ())), preferred_element_type=F32)


def unit_rows(projected):
    inverse = lax.rsqrt(jnp.sum(projected * projected, axis=-1, keepdims=True) + EPSILON)
    return (projected * inverse, inverse)


def back_unit(gradient, unit, inverse):
    return (gradient - unit * jnp.sum(unit * gradient, axis=-1, keepdims=True)) * inverse


def copy(source, target, sem):
    moving = pltpu.make_async_copy(source, target, sem)
    moving.start()
    return moving


def text_kernel(len_ref, x_ref, w_ref, out_ref):
    unit, _ = unit_rows(jnp.dot(x_ref[...], w_ref[...], preferred_element_type=F32))
    half = unit.astype(BF16)
    rows, width = half.shape
    line = lax.broadcasted_iota(jnp.int32, (8, width), 0)
    lens = jnp.where(line == 0, len_ref[0], len_ref[1]).astype(F32).astype(BF16)
    for d in range(out_ref.shape[0]):
        out_ref[d, :rows, :] = half
        out_ref[d, rows:, :] = lens


def unit_kernel(x_ref, w_ref, unit_ref, inv_ref):
    unit, inverse = unit_rows(jnp.dot(x_ref[...], w_ref[...], preferred_element_type=F32))
    unit_ref[...] = unit
    inv_ref[...] = jnp.broadcast_to(inverse, inv_ref.shape)


def image_kernel(x_ref, w_ref, half_ref):
    unit, _ = unit_rows(jnp.dot(x_ref[...], w_ref[...], preferred_element_type=F32))
    half_ref[...] = unit.astype(BF16)


def score_kernel(text_len, img_len, g_ref, half_ref, wt_hbm, stats_hbm, wt_ref, pooled_ref, logits_ref, wt_sem, sem):
    owners = g_ref.shape[0]
    rows = 2 * text_len
    columns = half_ref.shape[0]
    half = half_ref[...]
    token = lax.broadcasted_iota(jnp.int32, (text_len, 128), 0).astype(F32)
    pooled_ref[...] = jnp.zeros_like(pooled_ref)
    moving = []
    for d in range(owners):
        scores = along_last(g_ref[d, :rows, :], half)
        lens = g_ref[d, rows:, :128].astype(F32)
        for j in range(2):
            keep = token < lens[j : j + 1, :]
            keep = jnp.concatenate([keep] * (columns // 128), axis=1)
            own = jnp.where(keep, scores[j * text_len : (j + 1) * text_len], LOW)
            top = jnp.max(own, axis=0, keepdims=True)
            expos = jnp.exp2((own - top) * (TOKEN_SCALE * LOG2E))
            total = jnp.sum(expos, axis=0, keepdims=True)
            b = 2 * d + j
            wt_ref[b * text_len : (b + 1) * text_len, :] = (expos * (1.0 / total)).astype(BF16)
            pooled_ref[b : b + 1, :] = top + jnp.log(total) / TOKEN_SCALE
        part = pl.ds(d * rows, rows)
        moving.append(copy(wt_ref.at[part, :], wt_hbm.at[part, :], wt_sem.at[d]))
    lane = lax.broadcasted_iota(jnp.int32, (128, 128), 1)
    first = jnp.sum(pooled_ref[:, :img_len], axis=1, keepdims=True)
    second = jnp.sum(pooled_ref[:, img_len:], axis=1, keepdims=True)
    table = jnp.where(lane == 0, first, second) * (PAIR_SCALE / img_len)
    logits = table.T[:8, :]
    line = lax.broadcasted_iota(jnp.int32, logits.shape, 0)
    logits_ref[...] = jnp.where(line < 2, logits, LOW)
    moving += [copy(logits_ref, stats_hbm.at[d], sem.at[d]) for d in range(owners)]
    for one in moving:
        one.wait()


def pair_kernel(
    group_size, img_len, pairs_ref, all_ref, own_ref, half_ref, wt_hbm, pay_hbm, pair_hbm,
    wt_ref, pair_ref, pay_ref, wt_sem, pair_sem, sem,
):
    owners = all_ref.shape[0]
    text_len = pay_ref.shape[1] // 2
    rows = wt_hbm.shape[0] // 3
    weights = [
        copy(wt_hbm.at[pl.ds(k * rows, rows), :], wt_ref.at[pl.ds(k * rows, rows), :], wt_sem.at[k]) for k in range(3)
    ]
    start = (lax.axis_index("neg_0") * lax.axis_size("neg_1") + lax.axis_index("neg_1")) * 2
    everyone = all_ref[...].reshape(owners * 8, 128)
    col_top = jnp.max(everyone, axis=0, keepdims=True)
    col_sum = jnp.sum(jnp.exp(everyone - col_top), axis=0, keepdims=True)
    own = own_ref[0]
    lane = lax.broadcasted_iota(jnp.int32, own.shape, 1)
    line = lax.broadcasted_iota(jnp.int32, own.shape, 0)
    row = jnp.where(lane < group_size, own, LOW)
    expos = jnp.exp(row - jnp.max(row, axis=1, keepdims=True))
    row_prob = expos / jnp.sum(expos, axis=1, keepdims=True)
    col_prob = jnp.exp(own - col_top) / col_sum
    target = (lane == jnp.where(line == 0, pairs_ref[0, start], pairs_ref[0, start + 1])).astype(F32)
    pair = (row_prob + col_prob - 2.0 * target) * (PAIR_SCALE / (2.0 * group_size * img_len))
    pair = jnp.concatenate([pair, jnp.zeros((120, 128), F32)], axis=0).T
    pair_ref[...] = pair
    moving = [copy(pair_ref, pair_hbm.at[0], pair_sem)]
    for k in range(3):
        weights[k].wait()
        first = jnp.dot(wt_ref[k * rows : (k + 1) * rows, :img_len], half_ref[:img_len, :], preferred_element_type=F32)
        second = jnp.dot(wt_ref[k * rows : (k + 1) * rows, img_len:], half_ref[img_len:, :], preferred_element_type=F32)
        for b in range(k * rows // text_len, (k + 1) * rows // text_len):
            part = slice(b * text_len - k * rows, (b + 1) * text_len - k * rows)
            both = first[part] * pair[b : b + 1, 0:1] + second[part] * pair[b : b + 1, 1:2]
            d, j = b // 2, b % 2
            pay_ref[d, j * text_len : (j + 1) * text_len, :] = both.astype(BF16)
            if j:
                moving.append(copy(pay_ref.at[d], pay_hbm.at[d], sem.at[d]))
    for one in moving:
        one.wait()


def image_back_kernel(
    text_len, pair_hbm, g_hbm, wt_hbm, w_hbm, x_hbm, back_hbm, *refs
):
    turned, refs = refs[:4], refs[4:]
    pair_ref, g_ref, wt_ref, w_ref, x_ref, scaled_ref, back_ref, pay_ref, in_sem, out_sem = refs
    owners = g_ref.shape[0]
    pair = copy(pair_hbm.at[0], pair_ref, in_sem.at[4])
    group = copy(g_hbm, g_ref, in_sem.at[0])
    image = copy(x_hbm, x_ref, in_sem.at[1])
    projection = copy(w_hbm, w_ref, in_sem.at[2])
    weights = copy(wt_hbm, wt_ref, in_sem.at[3])
    img_len = x_ref.shape[0] // 2
    pair.wait()
    group.wait()
    for a in range(2):
        for b in range(2 * owners):
            text = g_ref[b // 2, (b % 2) * text_len : (b % 2 + 1) * text_len, :].astype(F32)
            scaled = text * pair_ref[b : b + 1, a : a + 1]
            scaled_ref[a, b * text_len : (b + 1) * text_len, :] = scaled.astype(BF16)
    image.wait()
    projection.wait()
    unit, inverse = unit_rows(jnp.dot(x_ref[...], w_ref[...], preferred_element_type=F32))
    weights.wait()
    for a in range(2):
        part = slice(a * img_len, (a + 1) * img_len)
        gradient = along_rows(wt_ref[:, part], scaled_ref[a])
        back_ref[part, :] = back_unit(gradient, unit[part], inverse[part]).astype(BF16)
    result = copy(back_ref, back_hbm, out_sem.at[4])
    tiles = along_rows(x_ref[...], back_ref[...]).reshape(-1, 16, back_ref.shape[1])
    for j in range(4):
        h, k = j // 2, j % 2
        piece = tiles[:, 8 * h : 8 * h + 8, 128 * k : 128 * k + 128]
        pay_ref[j] = piece.reshape(pay_ref.shape[1:]).astype(BF16)
    me = lax.axis_index("neg_1")
    moving = [
        copy(pay_ref.at[lax.rem(me + turn, 4)], target, out_sem.at[turn]) for turn, target in enumerate(turned)
    ]
    for one in moving:
        one.wait()
    result.wait()


def text_back_kernel(all_ref, unit_ref, inv_ref, x_ref, back_ref, pay_ref):
    gradient = all_ref[0].astype(F32)
    for d in range(1, all_ref.shape[0]):
        gradient += all_ref[d].astype(F32)
    back = back_unit(gradient, unit_ref[...], inv_ref[:, :1]).astype(BF16)
    back_ref[...] = back
    tiles = along_rows(x_ref[...], back).reshape(-1, 16, back.shape[1])
    for j in range(4):
        h, k = j // 2, j % 2
        piece = tiles[:, 8 * h : 8 * h + 8, 128 * k : 128 * k + 128]
        pay_ref[j] = piece.reshape(pay_ref.shape[1:]).astype(BF16)


def feature_kernel(img_ref, w_img_ref, txt_ref, w_txt_ref, img_out, txt_out):
    img_out[...] = along_last(img_ref[...], w_img_ref[...]).astype(BF16)
    txt_out[...] = along_last(txt_ref[...], w_txt_ref[...]).astype(BF16)


def partial_kernel(*refs):
    images, txt_ref, out_ref = refs[:-2], refs[-2], refs[-1]
    groups = ([r[...] for r in images], [txt_ref[d] for d in range(txt_ref.shape[0])])
    for k, parts in enumerate(groups):
        total = parts[0].astype(F32)
        for part in parts[1:]:
            total += part.astype(F32)
        out_ref[:, 8 * k : 8 * k + 8, :] = total.astype(BF16).reshape(out_ref.shape[0], 8, 128)


def rows_kernel(all_ref, out_ref):
    total = jnp.sum(all_ref[...].astype(F32), axis=0)
    for d in range(out_ref.shape[0]):
        out_ref[d] = total


def final_kernel(outer, all_ref, img_ref, txt_ref):
    inner = all_ref.shape[0] // outer
    for j in range(inner):
        total = all_ref[j]
        for i in range(1, outer):
            total += all_ref[i * inner + j]
        h, k = j // 2, j % 2
        img_ref[8 * h : 8 * h + 8, 128 * k : 128 * k + 128] = total[:8]
        txt_ref[8 * h : 8 * h + 8, 128 * k : 128 * k + 128] = total[8:]


def swap(array, axis):
    return lax.all_to_all(array, axis, 0, 0, tiled=True)


def window(img_features, txt_features, w_img, w_txt, cap_len, pairs):
    local_count, img_len, depth = img_features.shape
    text_len = txt_features.shape[1]
    width = w_img.shape[1]
    owners = lax.axis_size(NEG)
    outer = lax.axis_size("neg_0")
    dp = lax.axis_size("dp")
    group_size = owners * local_count
    img_rows, txt_rows = local_count * img_len, local_count * text_len
    img_flat = img_features.reshape(img_rows, depth)
    txt_flat = txt_features.reshape(txt_rows, depth)
    DMA = pltpu.SemaphoreType.DMA

    (sent,) = call(
        text_kernel,
        [shape((owners, txt_rows + 8, width), BF16)],
        [SMEM, VMEM, VMEM],
        2 * txt_rows * depth * width,
        grant=63,
    )(cap_len, txt_flat, w_txt)
    group = swap(sent, NEG)
    (img_half,) = call(
        image_kernel, [shape((img_rows, width), BF16)], [VMEM, VMEM], 2 * img_rows * depth * width
    )(img_flat, w_img)
    weights, own = call(
        lambda *refs: score_kernel(text_len, img_len, *refs),
        [shape((group_size * text_len, img_rows), BF16), shape((owners, 8, 128), F32)],
        [VMEM, VMEM],
        2 * group_size * text_len * img_rows * width,
        [
            pltpu.VMEM((group_size * text_len, img_rows), BF16),
            pltpu.VMEM((128, img_rows), F32),
            pltpu.VMEM((8, 128), F32),
            DMA((owners,)),
            DMA((owners,)),
        ],
        places=[HBM, HBM],
        grant=SCORE_GRANT,
    )(group, img_half)
    everyone = swap(own, NEG)
    text_terms, pair = call(
        lambda *refs: pair_kernel(group_size, img_len, *refs),
        [shape((owners, txt_rows, width), BF16), shape((32, 128, 128), F32)],
        [SMEM, VMEM, VMEM, VMEM, HBM],
        2 * group_size * text_len * img_rows * width,
        [
            pltpu.VMEM((group_size * text_len, img_rows), BF16),
            pltpu.VMEM((128, 128), F32),
            pltpu.VMEM((owners, txt_rows, width), BF16),
            DMA((3,)),
            DMA,
            DMA((owners,)),
        ],
        places=[HBM, HBM],
        grant=PAIR_GRANT,
    )(pairs, everyone, own, img_half, weights)
    arrived = swap(text_terms, NEG)
    img_back, *turned = call(
        lambda *refs: image_back_kernel(text_len, *refs),
        [shape((img_rows, width), BF16)] + [shape((depth // 2, 128), BF16)] * 4,
        [HBM, HBM, HBM, HBM, HBM],
        2 * img_rows * width * (group_size * text_len + depth),
        [
            pltpu.VMEM((128, 128), F32),
            pltpu.VMEM((owners, txt_rows + 8, width), BF16),
            pltpu.VMEM((group_size * text_len, img_rows), BF16),
            pltpu.VMEM((depth, width), BF16),
            pltpu.VMEM((img_rows, depth), BF16),
            pltpu.VMEM((2, group_size * text_len, width), BF16),
            pltpu.VMEM((img_rows, width), BF16),
            pltpu.VMEM((4, depth // 2, 128), BF16),
            DMA((5,)),
            DMA((5,)),
        ],
        places=[HBM] * 5,
        grant=BACK_GRANT,
    )(pair, group, weights, w_img, img_flat)
    for turn in range(1, 4):
        turned[turn] = lax.ppermute(turned[turn], "neg_1", [(k, (k + turn) % 4) for k in range(4)])
    txt_unit, txt_inv = call(
        unit_kernel,
        [shape((txt_rows, width), F32), shape((txt_rows, 128), F32)],
        [VMEM, VMEM],
        2 * txt_rows * width * depth,
    )(txt_flat, w_txt)
    txt_back, txt_pieces = call(
        text_back_kernel,
        [shape((txt_rows, width), BF16), shape((4, depth // 2, 128), BF16)],
        [VMEM] * 4,
        2 * txt_rows * width * depth,
    )(arrived, txt_unit, txt_inv, txt_flat)
    txt_quarter = swap(txt_pieces, "neg_1")
    (partial,) = call(partial_kernel, [shape((dp, 16, 128), BF16)], [VMEM] * 5, 8 * depth * 64)(
        *turned, txt_quarter
    )
    everything = swap(partial, "dp")
    (mine,) = call(rows_kernel, [shape((owners, 16, 128), F32)], [VMEM], 2 * dp * 2048)(everything)
    feat_img, feat_txt = call(
        feature_kernel,
        [shape((img_rows, depth), BF16), shape((txt_rows, depth), BF16)],
        [VMEM] * 4,
        2 * (img_rows + txt_rows) * depth * width,
        grant=FEATURE_GRANT,
    )(img_back, w_img, txt_back, w_txt)
    final_img, final_txt = call(
        lambda *refs: final_kernel(outer, *refs),
        [shape((16, width), F32), shape((16, width), F32)],
        [VMEM],
        owners * 2048,
    )(swap(mine, NEG))
    return (
        feat_img.reshape(img_features.shape),
        feat_txt.reshape(txt_features.shape),
        final_img,
        final_txt,
    )


def solution(mesh):
    split = Mesh(mesh.devices.reshape(mesh.shape["dp"], 3, 4), ("dp", "neg_0", "neg_1"))
    return jax.shard_map(
        window,
        mesh=split,
        in_specs=(P(DP_NEG, None, None), P(DP_NEG, None, None), P(), P(), P(DP_NEG), P("dp", None)),
        out_specs=(P(DP_NEG, None, None), P(DP_NEG, None, None), P("dp", None), P("dp", None)),
        check_vma=False,
    )
```

```python
import jax
import jax.numpy as jnp
from jax import lax
from jax.experimental import pallas as pl
from jax.experimental.pallas import tpu as pltpu
from jax.sharding import Mesh
from jax.sharding import PartitionSpec as P

NEG = ("neg_0", "neg_1")
DP_NEG = ("dp", "neg_0", "neg_1")

TOKEN_SCALE = 100.0
PAIR_SCALE = 50.0
EPSILON = 1e-06
LOG2E = 1.4426950408889634
LOW = -1e30
SCORE_GRANT = 52
PAIR_GRANT = 52
BACK_GRANT = 53
FEATURE_GRANT = 53
F32 = jnp.float32
BF16 = jnp.bfloat16

VMEM = pl.BlockSpec(memory_space=pltpu.VMEM)
SMEM = pl.BlockSpec(memory_space=pltpu.SMEM)
HBM = pl.BlockSpec(memory_space=pltpu.HBM)


def call(kernel, outs, specs, flops, scratch=(), grant=8, places=None):
    moved = sum(o.size * o.dtype.itemsize for o in outs)
    return pl.pallas_call(
        kernel,
        out_shape=tuple(outs),
        in_specs=specs,
        out_specs=tuple(places or [VMEM] * len(outs)),
        scratch_shapes=list(scratch),
        cost_estimate=pl.CostEstimate(flops=flops, bytes_accessed=2 * moved, transcendentals=0),
        compiler_params=pltpu.CompilerParams(vmem_limit_bytes=int(grant * 2**20)),
    )


def shape(dims, dtype):
    return jax.ShapeDtypeStruct(dims, dtype)


def along_rows(a, b):
    return lax.dot_general(a, b, (((0,), (0,)), ((), ())), preferred_element_type=F32)


def along_last(a, b):
    return lax.dot_general(a, b, (((1,), (1,)), ((), ())), preferred_element_type=F32)


def unit_rows(projected):
    inverse = lax.rsqrt(jnp.sum(projected * projected, axis=-1, keepdims=True) + EPSILON)
    return (projected * inverse, inverse)


def back_unit(gradient, unit, inverse):
    return (gradient - unit * jnp.sum(unit * gradient, axis=-1, keepdims=True)) * inverse


def copy(source, target, sem):
    moving = pltpu.make_async_copy(source, target, sem)
    moving.start()
    return moving


def text_kernel(len_ref, x_ref, w_ref, out_ref):
    unit, _ = unit_rows(jnp.dot(x_ref[...], w_ref[...], preferred_element_type=F32))
    half = unit.astype(BF16)
    rows, width = half.shape
    line = lax.broadcasted_iota(jnp.int32, (8, width), 0)
    lens = jnp.where(line == 0, len_ref[0], len_ref[1]).astype(F32).astype(BF16)
    for d in range(out_ref.shape[0]):
        out_ref[d, :rows, :] = half
        out_ref[d, rows:, :] = lens


def unit_kernel(x_ref, w_ref, unit_ref, inv_ref):
    unit, inverse = unit_rows(jnp.dot(x_ref[...], w_ref[...], preferred_element_type=F32))
    unit_ref[...] = unit
    inv_ref[...] = jnp.broadcast_to(inverse, inv_ref.shape)


def image_kernel(x_ref, w_ref, half_ref):
    unit, _ = unit_rows(jnp.dot(x_ref[...], w_ref[...], preferred_element_type=F32))
    half_ref[...] = unit.astype(BF16)


def score_kernel(text_len, img_len, g_ref, half_ref, wt_hbm, stats_hbm, wt_ref, pooled_ref, logits_ref, wt_sem, sem):
    owners = g_ref.shape[0]
    rows = 2 * text_len
    columns = half_ref.shape[0]
    half = half_ref[...]
    token = lax.broadcasted_iota(jnp.int32, (text_len, 128), 0).astype(F32)
    pooled_ref[...] = jnp.zeros_like(pooled_ref)
    moving = []
    for d in range(owners):
        scores = along_last(g_ref[d, :rows, :], half)
        lens = g_ref[d, rows:, :128].astype(F32)
        for j in range(2):
            keep = token < lens[j : j + 1, :]
            keep = jnp.concatenate([keep] * (columns // 128), axis=1)
            own = jnp.where(keep, scores[j * text_len : (j + 1) * text_len], LOW)
            top = jnp.max(own, axis=0, keepdims=True)
            expos = jnp.exp2((own - top) * (TOKEN_SCALE * LOG2E))
            total = jnp.sum(expos, axis=0, keepdims=True)
            b = 2 * d + j
            wt_ref[b * text_len : (b + 1) * text_len, :] = (expos * (1.0 / total)).astype(BF16)
            pooled_ref[b : b + 1, :] = top + jnp.log(total) / TOKEN_SCALE
        part = pl.ds(d * rows, rows)
        moving.append(copy(wt_ref.at[part, :], wt_hbm.at[part, :], wt_sem.at[d]))
    lane = lax.broadcasted_iota(jnp.int32, (128, 128), 1)
    first = jnp.sum(pooled_ref[:, :img_len], axis=1, keepdims=True)
    second = jnp.sum(pooled_ref[:, img_len:], axis=1, keepdims=True)
    table = jnp.where(lane == 0, first, second) * (PAIR_SCALE / img_len)
    logits = table.T[:8, :]
    line = lax.broadcasted_iota(jnp.int32, logits.shape, 0)
    logits_ref[...] = jnp.where(line < 2, logits, LOW)
    moving += [copy(logits_ref, stats_hbm.at[d], sem.at[d]) for d in range(owners)]
    for one in moving:
        one.wait()


def pair_kernel(
    group_size, img_len, pairs_ref, all_ref, own_ref, half_ref, wt_hbm, pay_hbm, pair_hbm,
    wt_ref, pair_ref, pay_ref, wt_sem, pair_sem, sem,
):
    owners = all_ref.shape[0]
    text_len = pay_ref.shape[1] // 2
    rows = wt_hbm.shape[0] // 3
    weights = [
        copy(wt_hbm.at[pl.ds(k * rows, rows), :], wt_ref.at[pl.ds(k * rows, rows), :], wt_sem.at[k]) for k in range(3)
    ]
    start = (lax.axis_index("neg_0") * lax.axis_size("neg_1") + lax.axis_index("neg_1")) * 2
    everyone = all_ref[...].reshape(owners * 8, 128)
    col_top = jnp.max(everyone, axis=0, keepdims=True)
    col_sum = jnp.sum(jnp.exp(everyone - col_top), axis=0, keepdims=True)
    own = own_ref[0]
    lane = lax.broadcasted_iota(jnp.int32, own.shape, 1)
    line = lax.broadcasted_iota(jnp.int32, own.shape, 0)
    row = jnp.where(lane < group_size, own, LOW)
    expos = jnp.exp(row - jnp.max(row, axis=1, keepdims=True))
    row_prob = expos / jnp.sum(expos, axis=1, keepdims=True)
    col_prob = jnp.exp(own - col_top) / col_sum
    target = (lane == jnp.where(line == 0, pairs_ref[0, start], pairs_ref[0, start + 1])).astype(F32)
    pair = (row_prob + col_prob - 2.0 * target) * (PAIR_SCALE / (2.0 * group_size * img_len))
    pair = jnp.concatenate([pair, jnp.zeros((120, 128), F32)], axis=0).T
    pair_ref[...] = pair
    moving = [copy(pair_ref, pair_hbm.at[0], pair_sem)]
    for k in range(3):
        weights[k].wait()
        first = jnp.dot(wt_ref[k * rows : (k + 1) * rows, :img_len], half_ref[:img_len, :], preferred_element_type=F32)
        second = jnp.dot(wt_ref[k * rows : (k + 1) * rows, img_len:], half_ref[img_len:, :], preferred_element_type=F32)
        for b in range(k * rows // text_len, (k + 1) * rows // text_len):
            part = slice(b * text_len - k * rows, (b + 1) * text_len - k * rows)
            both = first[part] * pair[b : b + 1, 0:1] + second[part] * pair[b : b + 1, 1:2]
            d, j = b // 2, b % 2
            pay_ref[d, j * text_len : (j + 1) * text_len, :] = both.astype(BF16)
            if j:
                moving.append(copy(pay_ref.at[d], pay_hbm.at[d], sem.at[d]))
    for one in moving:
        one.wait()


def image_back_kernel(
    text_len, pair_hbm, g_hbm, wt_hbm, w_hbm, x_hbm, back_hbm, *refs
):
    kept, given, refs = refs[0], refs[1], refs[2:]
    pair_ref, g_ref, wt_ref, w_ref, x_ref, scaled_ref, back_ref, pay_ref, in_sem, out_sem = refs
    owners = g_ref.shape[0]
    pair = copy(pair_hbm.at[0], pair_ref, in_sem.at[4])
    group = copy(g_hbm, g_ref, in_sem.at[0])
    image = copy(x_hbm, x_ref, in_sem.at[1])
    projection = copy(w_hbm, w_ref, in_sem.at[2])
    weights = copy(wt_hbm, wt_ref, in_sem.at[3])
    img_len = x_ref.shape[0] // 2
    pair.wait()
    group.wait()
    for a in range(2):
        for b in range(2 * owners):
            text = g_ref[b // 2, (b % 2) * text_len : (b % 2 + 1) * text_len, :].astype(F32)
            scaled = text * pair_ref[b : b + 1, a : a + 1]
            scaled_ref[a, b * text_len : (b + 1) * text_len, :] = scaled.astype(BF16)
    image.wait()
    projection.wait()
    unit, inverse = unit_rows(jnp.dot(x_ref[...], w_ref[...], preferred_element_type=F32))
    weights.wait()
    for a in range(2):
        part = slice(a * img_len, (a + 1) * img_len)
        gradient = along_rows(wt_ref[:, part], scaled_ref[a])
        back_ref[part, :] = back_unit(gradient, unit[part], inverse[part]).astype(BF16)
    result = copy(back_ref, back_hbm, out_sem.at[4])
    tiles = along_rows(x_ref[...], back_ref[...]).reshape(-1, 16, back_ref.shape[1])
    for j in range(4):
        h, k = j // 2, j % 2
        piece = tiles[:, 8 * h : 8 * h + 8, 128 * k : 128 * k + 128]
        pay_ref[k, h] = piece.reshape(-1, 128).astype(BF16)
    mine = lax.rem(lax.axis_index("dp"), 2)
    moving = [copy(pay_ref.at[mine], kept, out_sem.at[0]), copy(pay_ref.at[1 - mine], given, out_sem.at[1])]
    for one in moving:
        one.wait()
    result.wait()


def text_back_kernel(all_ref, unit_ref, inv_ref, x_ref, back_ref, pay_ref):
    gradient = all_ref[0].astype(F32)
    for d in range(1, all_ref.shape[0]):
        gradient += all_ref[d].astype(F32)
    back = back_unit(gradient, unit_ref[...], inv_ref[:, :1]).astype(BF16)
    back_ref[...] = back
    tiles = along_rows(x_ref[...], back).reshape(-1, 16, back.shape[1])
    for j in range(4):
        h, k = j // 2, j % 2
        piece = tiles[:, 8 * h : 8 * h + 8, 128 * k : 128 * k + 128]
        pay_ref[j] = piece.reshape(pay_ref.shape[1:]).astype(BF16)


def half_kernel(kept_ref, given_ref, mine_ref, next_ref):
    side = lax.rem(lax.axis_index("dp") // 2, 2)
    mine_ref[...] = (kept_ref[side].astype(F32) + given_ref[side].astype(F32)).astype(BF16)
    next_ref[...] = (kept_ref[1 - side].astype(F32) + given_ref[1 - side].astype(F32)).astype(BF16)


def feature_kernel(img_ref, w_img_ref, txt_ref, w_txt_ref, img_out, txt_out):
    img_out[...] = along_last(img_ref[...], w_img_ref[...]).astype(BF16)
    txt_out[...] = along_last(txt_ref[...], w_txt_ref[...]).astype(BF16)


def partial_kernel(*refs):
    images, txt_ref, out_ref = refs[:-2], refs[-2], refs[-1]
    groups = ([r[...] for r in images], [txt_ref[d] for d in range(txt_ref.shape[0])])
    for k, parts in enumerate(groups):
        total = parts[0].astype(F32)
        for part in parts[1:]:
            total += part.astype(F32)
        out_ref[:, 8 * k : 8 * k + 8, :] = total.astype(BF16).reshape(out_ref.shape[0], 8, 128)


def rows_kernel(all_ref, out_ref):
    img = jnp.sum(all_ref[:, :8, :].astype(F32).reshape(-1, 4, 8, 128), axis=0).reshape(32, 128)
    txt = jnp.sum(all_ref[:, 8:, :].astype(F32), axis=0)
    for d in range(out_ref.shape[0]):
        out_ref[d, :32, :] = img.astype(BF16)
        out_ref[d, 32:, :] = txt.astype(BF16)


def final_kernel(outer, all_ref, img_ref, txt_ref):
    inner = all_ref.shape[0] // outer
    img = jnp.sum(all_ref[:, :32, :].astype(F32), axis=0)
    for j in range(inner):
        txt = all_ref[j, 32:].astype(F32)
        for i in range(1, outer):
            txt += all_ref[i * inner + j, 32:].astype(F32)
        h, k = j // 2, j % 2
        img_ref[8 * h : 8 * h + 8, 128 * k : 128 * k + 128] = img[8 * j : 8 * j + 8]
        txt_ref[8 * h : 8 * h + 8, 128 * k : 128 * k + 128] = txt


def swap(array, axis):
    return lax.all_to_all(array, axis, 0, 0, tiled=True)


def window(img_features, txt_features, w_img, w_txt, cap_len, pairs):
    local_count, img_len, depth = img_features.shape
    text_len = txt_features.shape[1]
    width = w_img.shape[1]
    owners = lax.axis_size(NEG)
    outer = lax.axis_size("neg_0")
    dp = lax.axis_size("dp")
    group_size = owners * local_count
    img_rows, txt_rows = local_count * img_len, local_count * text_len
    img_flat = img_features.reshape(img_rows, depth)
    txt_flat = txt_features.reshape(txt_rows, depth)
    DMA = pltpu.SemaphoreType.DMA

    (sent,) = call(
        text_kernel,
        [shape((owners, txt_rows + 8, width), BF16)],
        [SMEM, VMEM, VMEM],
        2 * txt_rows * depth * width,
        grant=63,
    )(cap_len, txt_flat, w_txt)
    group = swap(sent, NEG)
    (img_half,) = call(
        image_kernel, [shape((img_rows, width), BF16)], [VMEM, VMEM], 2 * img_rows * depth * width
    )(img_flat, w_img)
    weights, own = call(
        lambda *refs: score_kernel(text_len, img_len, *refs),
        [shape((group_size * text_len, img_rows), BF16), shape((owners, 8, 128), F32)],
        [VMEM, VMEM],
        2 * group_size * text_len * img_rows * width,
        [
            pltpu.VMEM((group_size * text_len, img_rows), BF16),
            pltpu.VMEM((128, img_rows), F32),
            pltpu.VMEM((8, 128), F32),
            DMA((owners,)),
            DMA((owners,)),
        ],
        places=[HBM, HBM],
        grant=SCORE_GRANT,
    )(group, img_half)
    everyone = swap(own, NEG)
    text_terms, pair = call(
        lambda *refs: pair_kernel(group_size, img_len, *refs),
        [shape((owners, txt_rows, width), BF16), shape((32, 128, 128), F32)],
        [SMEM, VMEM, VMEM, VMEM, HBM],
        2 * group_size * text_len * img_rows * width,
        [
            pltpu.VMEM((group_size * text_len, img_rows), BF16),
            pltpu.VMEM((128, 128), F32),
            pltpu.VMEM((owners, txt_rows, width), BF16),
            DMA((3,)),
            DMA,
            DMA((owners,)),
        ],
        places=[HBM, HBM],
        grant=PAIR_GRANT,
    )(pairs, everyone, own, img_half, weights)
    arrived = swap(text_terms, NEG)
    img_back, kept, given = call(
        lambda *refs: image_back_kernel(text_len, *refs),
        [shape((img_rows, width), BF16)] + [shape((2, depth // 2, 128), BF16)] * 2,
        [HBM, HBM, HBM, HBM, HBM],
        2 * img_rows * width * (group_size * text_len + depth),
        [
            pltpu.VMEM((128, 128), F32),
            pltpu.VMEM((owners, txt_rows + 8, width), BF16),
            pltpu.VMEM((group_size * text_len, img_rows), BF16),
            pltpu.VMEM((depth, width), BF16),
            pltpu.VMEM((img_rows, depth), BF16),
            pltpu.VMEM((2, group_size * text_len, width), BF16),
            pltpu.VMEM((img_rows, width), BF16),
            pltpu.VMEM((2, 2, depth // 2, 128), BF16),
            DMA((5,)),
            DMA((5,)),
        ],
        places=[HBM] * 3,
        grant=BACK_GRANT,
    )(pair, group, weights, w_img, img_flat)
    given = lax.ppermute(given, "dp", [(d, d ^ 1) for d in range(dp)])
    img_mine, img_given = call(
        half_kernel, [shape((depth // 2, 128), BF16)] * 2, [VMEM, VMEM], 2 * depth * 128
    )(kept, given)
    img_given = lax.ppermute(img_given, "dp", [(d, d ^ 2) for d in range(dp)])
    txt_unit, txt_inv = call(
        unit_kernel,
        [shape((txt_rows, width), F32), shape((txt_rows, 128), F32)],
        [VMEM, VMEM],
        2 * txt_rows * width * depth,
    )(txt_flat, w_txt)
    txt_back, txt_pieces = call(
        text_back_kernel,
        [shape((txt_rows, width), BF16), shape((4, depth // 2, 128), BF16)],
        [VMEM] * 4,
        2 * txt_rows * width * depth,
    )(arrived, txt_unit, txt_inv, txt_flat)
    txt_quarter = swap(txt_pieces, "neg_1")
    (partial,) = call(partial_kernel, [shape((dp, 16, 128), BF16)], [VMEM] * 3, 8 * depth * 64)(
        img_mine, img_given, txt_quarter
    )
    everything = swap(partial, "dp")
    (mine,) = call(rows_kernel, [shape((owners, 40, 128), BF16)], [VMEM], 2 * dp * 2048)(everything)
    feat_img, feat_txt = call(
        feature_kernel,
        [shape((img_rows, depth), BF16), shape((txt_rows, depth), BF16)],
        [VMEM] * 4,
        2 * (img_rows + txt_rows) * depth * width,
        grant=FEATURE_GRANT,
    )(img_back, w_img, txt_back, w_txt)
    final_img, final_txt = call(
        lambda *refs: final_kernel(outer, *refs),
        [shape((16, width), F32), shape((16, width), F32)],
        [VMEM],
        owners * 2048,
    )(swap(mine, NEG))
    return (
        feat_img.reshape(img_features.shape),
        feat_txt.reshape(txt_features.shape),
        final_img,
        final_txt,
    )


def solution(mesh):
    split = Mesh(mesh.devices.reshape(mesh.shape["dp"], 3, 4), ("dp", "neg_0", "neg_1"))
    return jax.shard_map(
        window,
        mesh=split,
        in_specs=(P(DP_NEG, None, None), P(DP_NEG, None, None), P(), P(), P(DP_NEG), P("dp", None)),
        out_specs=(P(DP_NEG, None, None), P(DP_NEG, None, None), P("dp", None), P("dp", None)),
        check_vma=False,
    )
```
